32 devices in a mesh: member: 2 (over x), tm: 4 (over z), tile: 4 (over y, core).
Axes of the slice: x: 2, y: 2, z: 4, core: 2. Of those that a mesh axis runs over, the one named last changes fastest.
Arguments:
- flux: bfloat16 [64, 32, 16384], P(('member', 'tm'), 'tile'), parts along dimension 0, may hold values from -6 to 6
- footprint: bfloat16 [4, 256, 4, 16384], P('tm', 'tile'), may hold values from 1.4424324e-05 to 0.014404297
- foot_slot: int32 [4, 256, 4], P('tm', 'tile'), may hold values from 0 to 7
- wanted: int32 [4, 4, 4, 2], P('tm', 'tile'), may hold values from 0 to 127
- counts: int32 [4, 4, 4], P('tm', 'tile'), may hold values from 1 to 2
- observed: float32 [4, 256], P('tm', 'tile'), may hold values from -6 to 6
- inv_var: float32 [4, 256], P('tm', 'tile'), may hold values from 25.6 to 102.4
Outputs:
- modeled: float32 [8, 256], P(('member', 'tm'), 'tile'), parts along dimension 0
- gradient: float32 [64, 32, 16384], P(('member', 'tm'), 'tile'), parts along dimension 0
The draws below stay inside these ranges and needn't reach their ends.
There are 2 independent parts, one for each index of `member`. The reference program is written for one: setup_inputs(seed, part) draws one part's arguments, and reference() takes and returns one part's arrays. A program takes and returns all parts, laid end to end along the dimension named above; an argument that names none is the same for every part. Nothing has to cross between parts.
All inputs are finite; a program needn't handle non-finite values.
Results may differ from the reference program's by a relative error of at most 0.0042.
Values may be sent and summed in bfloat16 or wider, within the bound.
A program may use at most 128 MiB of HBM per device.

```python
import math
import jax
import jax.numpy as jnp
import numpy as np
from jax import lax

TILE_CELLS = 16384
TW = 8
TILES_DEV = 8
NS = 64
K = 4
CAP = 2
TIMES = 32
TILES = 32
SOUNDINGS = 256
N_TM = 4
N_TILE = 4


def with_ends(drawn, own_key, least, largest):
    index_at = [jax.random.randint(jax.random.fold_in(own_key, axis), (), 0, length) for axis, length in enumerate(drawn.shape)]
    widest = drawn.shape.index(max(drawn.shape))
    beside = index_at[:widest] + [(index_at[widest] + 1) % drawn.shape[widest]] + index_at[widest + 1:]
    return drawn.at[tuple(index_at)].set(least).at[tuple(beside)].set(largest)


def level_of(own_key, extent, cuts, least, top_value):
    gain, own = 1.0, jax.random.fold_in(own_key, 6)
    for dim, parts in cuts:
        heights = jnp.exp(jax.random.uniform(jax.random.fold_in(own, dim), (parts,), jnp.float32, least / len(cuts), top_value / len(cuts)))
        gain = gain * jnp.repeat(heights, extent[dim] // parts).reshape([-1 if axis == dim else 1 for axis in range(len(extent))])
    return gain


def cumulative_ranks(amount, skew):
    weights = [(1 << 20) // math.isqrt(grade ** skew) + 1 for grade in range(1, amount + 1)]
    width = 1 + sum(weights) // (1 << 30)
    return np.cumsum(np.array([max(1, weight // width) for weight in weights]))


def ranked_ids(stream_key, dims, count, lean):
    grid = cumulative_ranks(count, lean)
    pick = jax.random.randint(jax.random.fold_in(stream_key, 1), dims, 0, int(grid[count - 1]))
    standing = jnp.searchsorted(jnp.asarray(grid, jnp.int32), pick, side="right")
    return jax.random.permutation(jax.random.fold_in(stream_key, 2), count)[standing].astype(jnp.int32)


def noise(stream_key, shape, width, limit, pieces=(), kind=jnp.bfloat16):
    loudness = level_of(stream_key, shape, pieces, -0.22, 0.18) if pieces else 1.0
    entries = jax.random.normal(stream_key, shape, jnp.float32) * width * loudness
    return jnp.minimum(jnp.maximum(entries, -limit), limit).astype(kind)


def setup_inputs(seed: int = 0, part: int = 0) -> dict:
    arg_keys = jax.random.split(jax.random.key(seed), 8)
    own_keys = jax.random.split(jax.random.fold_in(arg_keys[7], part), 8)
    return {
        "flux": noise(own_keys[0], (TIMES, TILES, TILE_CELLS), 1.0, 6.0, ((0, 4), (1, 4))),
        "footprint": jnp.clip(jnp.exp(math.log(0.014404297) - 6.906366 * jax.random.uniform(arg_keys[1], (N_TM, SOUNDINGS, K, TILE_CELLS), jnp.float32) ** level_of(arg_keys[1], (N_TM, SOUNDINGS, K, TILE_CELLS), ((0, 4), (1, 4)), -0.2, 0.2)), 1.4424324035644531e-05, 0.014404297).astype(jnp.bfloat16),
        "foot_slot": with_ends(ranked_ids(arg_keys[2], (N_TM, SOUNDINGS, K), N_TILE * CAP, 2), jax.random.fold_in(arg_keys[2], 3), 0, (N_TILE * CAP) - 1).astype(jnp.int32),
        "wanted": with_ends(jax.random.randint(arg_keys[3], (N_TM, N_TILE, N_TILE, CAP), 0, 2 * TW * TILES_DEV), jax.random.fold_in(arg_keys[3], 1), 0, (2 * TW * TILES_DEV) - 1).astype(jnp.int32),
        "counts": with_ends(jax.random.randint(arg_keys[4], (N_TM, N_TILE, N_TILE), 1, CAP + 1), jax.random.fold_in(arg_keys[4], 1), 1, CAP).astype(jnp.int32),
        "observed": noise(arg_keys[5], (N_TM, SOUNDINGS), 1.0, 6.0, ((0, 4), (1, 4)), jnp.float32),
        "inv_var": jnp.clip(jnp.exp(math.log(102.4) - 1.3862944 * jax.random.uniform(arg_keys[6], (N_TM, SOUNDINGS), jnp.float32) ** level_of(arg_keys[6], (N_TM, SOUNDINGS), ((0, 4), (1, 4)), -0.2, 0.2)), 25.6, 102.4),
    }


def reference(flux, footprint, foot_slot, wanted, counts, observed, inv_var):
    times, tiles, cells = flux.shape
    padded = jnp.concatenate([jnp.zeros((TW, tiles, cells), flux.dtype), flux], 0)
    owner_of = (jnp.arange(SOUNDINGS, dtype=jnp.int32) // NS).astype(jnp.int32)

    def window(grad, items):
        index, prints, entry, asked, have, measured, precision_w = items
        peer = entry // CAP
        place = entry % CAP
        asked_flat = asked.reshape(N_TILE, N_TILE * CAP)
        row = asked_flat[owner_of[:, None], entry]
        livef = (place < have[owner_of[:, None], peer]).astype(jnp.float32)
        step = (index * TW + row // TILES_DEV).astype(jnp.int32)
        tile = (peer * TILES_DEV + row % TILES_DEV).astype(jnp.int32)
        values = padded[step, tile].astype(jnp.float32)
        prints_f = prints.astype(jnp.float32)
        modeled = jnp.sum(livef[:, :, None] * prints_f * values, axis=(1, 2))
        coef = ((modeled - measured) * precision_w).astype(jnp.bfloat16)
        coef = lax.optimization_barrier(coef).astype(jnp.float32)
        contrib = prints_f * (coef[:, None] * livef)[:, :, None]
        grad = grad.at[step, tile].add(contrib)
        return grad, modeled

    start = jnp.zeros((times + TW, tiles, cells), jnp.float32)
    windows = jnp.arange(N_TM, dtype=jnp.int32)
    grad, modeled = lax.scan(window, start, (windows, footprint, foot_slot, wanted, counts, observed, inv_var))
    return modeled, grad[TW:]
```

```python
import jax
import jax.numpy as jnp
from jax import lax
from jax.experimental import pallas as pl
from jax.experimental.pallas import tpu as pltpu
from jax.sharding import PartitionSpec as P

MESH = pl.DeviceIdType.MESH
LANES = 128
CHUNKS = 4
BLOCKS = 8


def exchange_kernel(
    own_hbm, prints_hbm, slots_ref, wanted_ref, counts_ref, observed_ref, inv_var_ref,
    modeled_ref, returned_ref, hot_ref,
    own_buf, prints_buf, send_buf, recv_buf, adj_buf, asks, asked, scores,
    own_sem, prints_sem, self_sem, ask_send, ask_recv, out_send, out_recv, back_send, back_recv,
):
    windows, owners = lax.axis_size("tm"), lax.axis_size("tile")
    win, me = lax.axis_index("tm"), lax.axis_index("tile")
    steps_win, groups, tiles_dev, _ = own_hbm.shape
    soundings, _, per_sounding, _ = prints_hbm.shape
    capacity = wanted_ref.shape[0]
    own_rows = steps_win * tiles_dev
    entries = soundings * per_sounding
    slots = owners * capacity
    rows = 2 * slots
    chunks = own_sem.shape[0]
    per_chunk = groups // chunks
    has_before, has_after = win > 0, win < windows - 1

    own_rows_view = own_buf.reshape(groups, own_rows, LANES)
    prints_view = prints_buf.reshape(groups, entries, LANES)
    send_view = send_buf.reshape(groups, rows, LANES)
    recv_view = recv_buf.reshape(groups, rows, LANES)
    adj_view = adj_buf.reshape(groups, slots, LANES)
    returned_view = returned_ref.reshape(groups, rows, LANES)

    def span(chunk):
        return pl.ds(chunk * per_chunk, per_chunk)

    def remote(source, target, send, recv, window, tile):
        return pltpu.make_async_remote_copy(
            src_ref=source, dst_ref=target, send_sem=send, recv_sem=recv,
            device_id={"tm": window, "tile": tile}, device_id_type=MESH,
        )

    def others(step):
        for away in range(1, owners):
            step(lax.rem(me + away, owners))

    @pl.loop(0, groups)
    def _(group):
        pltpu.make_async_copy(
            own_hbm.at[:, group], own_buf.at[group], own_sem.at[group // per_chunk]
        ).start()

    barrier = pltpu.get_barrier_semaphore()

    def greet(window, tile):
        pl.semaphore_signal(barrier, inc=1, device_id={"tm": window, "tile": tile}, device_id_type=MESH)

    others(lambda tile: greet(win, tile))

    @pl.when(has_before)
    def _():
        for tile in range(owners):
            greet(win - 1, tile)

    @pl.when(has_after)
    def _():
        for tile in range(owners):
            greet(win + 1, tile)

    row_id = lax.broadcasted_iota(jnp.int32, asks.shape[2:], 0)
    for tile in range(owners):
        for late in range(2):
            block = jnp.full(asks.shape[2:], -1, jnp.int32)
            for place in range(capacity):
                value = wanted_ref[place, tile] - (0 if late else own_rows)
                block = jnp.where(row_id == (late * owners + me) * capacity + place, value, block)
            asks[late, tile] = block

    @pl.loop(0, groups)
    def _(group):
        pltpu.make_async_copy(
            prints_hbm.at[:, group], prints_buf.at[group], prints_sem.at[group // per_chunk]
        ).start()

    near = lax.div(win + windows - 1, windows) + lax.div(2 * windows - 2 - win, windows)
    pl.semaphore_wait(barrier, owners - 1 + owners * near)

    def ask(late, tile):
        return remote(
            asks.at[late, tile], asked.at[late * owners + me],
            ask_send.at[late * owners + tile], ask_recv.at[late * owners + me], win - late, tile,
        )

    def ask_from(late, tile):
        return remote(
            asks.at[late, tile], asked.at[late * owners + tile],
            ask_send.at[late * owners + tile], ask_recv.at[late * owners + tile], win, me,
        )

    @pl.when(has_before)
    def _():
        for tile in range(owners):
            ask(1, tile).start()

    others(lambda tile: ask(0, tile).start())
    asked[me] = asks[0, me]

    @pl.when(jnp.logical_not(has_after))
    def _():
        asked[owners:] = jnp.full((owners,) + asked.shape[1:], -1, jnp.int32)

    @pl.when(jnp.logical_not(has_before))
    def _():
        @pl.loop(0, groups)
        def _(group):
            recv_buf[group, owners:] = jnp.zeros((owners, capacity, LANES), jnp.bfloat16)

    others(lambda tile: ask_from(0, tile).wait_recv())

    @pl.when(has_after)
    def _():
        for tile in range(owners):
            ask_from(1, tile).wait_recv()

    value = asked[0]
    for index in range(1, 2 * owners):
        value = jnp.maximum(value, asked[index])
    value = value[:, :own_rows]
    hot = (value == lax.broadcasted_iota(jnp.int32, value.shape, 1)).astype(jnp.float32).astype(jnp.bfloat16)
    hot_ref[...] = hot

    def out(chunk, late, tile):
        return remote(
            send_buf.at[span(chunk), late * owners + tile], recv_buf.at[span(chunk), late * owners + me],
            out_send.at[chunk, late * owners + tile], out_recv.at[chunk, late * owners + me], win + late, tile,
        )

    def out_from(chunk, late, tile):
        return remote(
            send_buf.at[span(chunk), late * owners + tile], recv_buf.at[span(chunk), late * owners + tile],
            out_send.at[chunk, late * owners + tile], out_recv.at[chunk, late * owners + tile], win, me,
        )

    def out_self(chunk):
        return pltpu.make_async_copy(
            send_buf.at[span(chunk), me], recv_buf.at[span(chunk), me], self_sem.at[0, chunk]
        )

    @pl.loop(0, chunks)
    def _(chunk):
        own_part = own_buf.at[span(chunk)]
        pltpu.make_async_copy(own_part, own_part, own_sem.at[chunk]).wait()

        @pl.loop(0, per_chunk // 2, unroll=4)
        def _(step):
            group = chunk * per_chunk + 2 * step
            pair = jnp.concatenate([own_rows_view[group], own_rows_view[group + 1]], axis=1)
            picked = jnp.dot(hot, pair, preferred_element_type=jnp.float32).astype(jnp.bfloat16)
            send_view[group] = picked[:, :LANES]
            send_view[group + 1] = picked[:, LANES:]

        @pl.when(has_after)
        def _():
            for tile in range(owners):
                out(chunk, 1, tile).start()

        others(lambda tile: out(chunk, 0, tile).start())
        out_self(chunk).start()

    scores[...] = jnp.zeros_like(scores)

    @pl.loop(0, chunks)
    def _(chunk):
        prints_part = prints_buf.at[span(chunk)]
        pltpu.make_async_copy(prints_part, prints_part, prints_sem.at[chunk]).wait()
        others(lambda tile: out_from(chunk, 0, tile).wait_recv())
        out_self(chunk).wait()

        @pl.when(has_before)
        def _():
            for tile in range(owners):
                out_from(chunk, 1, tile).wait_recv()

        def score(step, total):
            group = chunk * per_chunk + 2 * step
            pair = jnp.concatenate([prints_view[group], prints_view[group + 1]], axis=1)
            held = jnp.concatenate([recv_view[group], recv_view[group + 1]], axis=1)
            return total + lax.dot_general(
                held, pair, (((1,), (1,)), ((), ())), preferred_element_type=jnp.float32
            )

        scores[...] = lax.fori_loop(0, per_chunk // 2, score, scores[...], unroll=4)

    low = lax.broadcasted_iota(jnp.int32, (soundings, entries), 0) * per_sounding
    column = lax.broadcasted_iota(jnp.int32, (soundings, entries), 1)
    spread_of = ((column >= low) & (column < low + per_sounding)).astype(jnp.float32)
    each = jnp.dot(
        slots_ref[...].astype(jnp.float32), spread_of,
        precision=lax.Precision.HIGHEST, preferred_element_type=jnp.float32,
    )
    nth = lax.broadcasted_iota(jnp.int32, (per_sounding, entries), 0)
    at = lax.rem(lax.broadcasted_iota(jnp.int32, (per_sounding, entries), 1), per_sounding)
    entry = jnp.sum(jnp.where(nth == at, each, 0.0), axis=0, keepdims=True)
    slot_id = lax.broadcasted_iota(jnp.int32, (slots, entries), 0)
    have = jnp.zeros((slots, entries), jnp.int32)
    for tile in range(owners):
        have = jnp.where(slot_id // capacity == tile, counts_ref[0, tile], have)
    select = (slot_id.astype(jnp.float32) == entry) & (lax.rem(slot_id, capacity) < have)
    both = scores[:slots, :] + scores[slots:, :]
    entry_sums = jnp.sum(jnp.where(select, both, 0.0), axis=0, keepdims=True)
    modeled = lax.dot_general(
        jnp.broadcast_to(entry_sums, (8, entries)), spread_of, (((1,), (1,)), ((), ())),
        precision=lax.Precision.HIGHEST, preferred_element_type=jnp.float32,
    )
    modeled_ref[...] = modeled[:1]
    coef = ((modeled - observed_ref[...]) * inv_var_ref[...]).astype(jnp.bfloat16)
    coef_each = jnp.dot(coef, spread_of.astype(jnp.bfloat16), preferred_element_type=jnp.float32)[:1]
    weights = jnp.where(select, coef_each, 0.0).astype(jnp.bfloat16)

    def back(chunk, late, tile):
        return remote(
            adj_buf.at[span(chunk), tile], returned_ref.at[span(chunk), late * owners + me],
            back_send.at[chunk, late * owners + tile], back_recv.at[chunk, late * owners + me], win - late, tile,
        )

    def back_from(chunk, late, tile):
        return remote(
            adj_buf.at[span(chunk), tile], returned_ref.at[span(chunk), late * owners + tile],
            back_send.at[chunk, late * owners + tile], back_recv.at[chunk, late * owners + tile], win, me,
        )

    def back_self(chunk):
        return pltpu.make_async_copy(
            adj_buf.at[span(chunk), me], returned_ref.at[span(chunk), me], self_sem.at[1, chunk]
        )

    @pl.loop(0, chunks)
    def _(chunk):
        @pl.loop(0, per_chunk // 2, unroll=4)
        def _(step):
            group = chunk * per_chunk + 2 * step
            pair = jnp.concatenate([prints_view[group], prints_view[group + 1]], axis=1)
            adjoint = jnp.dot(weights, pair, preferred_element_type=jnp.float32).astype(jnp.bfloat16)
            adj_view[group] = adjoint[:, :LANES]
            adj_view[group + 1] = adjoint[:, LANES:]

        @pl.when(has_before)
        def _():
            for tile in range(owners):
                back(chunk, 1, tile).start()

        others(lambda tile: back(chunk, 0, tile).start())
        back_self(chunk).start()

    @pl.when(jnp.logical_not(has_after))
    def _():
        @pl.loop(0, groups)
        def _(group):
            returned_ref[group, owners:] = jnp.zeros((owners, capacity, LANES), jnp.bfloat16)

    others(lambda tile: ask(0, tile).wait_send())

    @pl.when(has_before)
    def _():
        for tile in range(owners):
            ask(1, tile).wait_send()

    @pl.loop(0, chunks)
    def _(chunk):
        others(lambda tile: out(chunk, 0, tile).wait_send())
        others(lambda tile: back(chunk, 0, tile).wait_send())
        others(lambda tile: back_from(chunk, 0, tile).wait_recv())
        back_self(chunk).wait()

        @pl.when(has_after)
        def _():
            for tile in range(owners):
                out(chunk, 1, tile).wait_send()
                back_from(chunk, 1, tile).wait_recv()

        @pl.when(has_before)
        def _():
            for tile in range(owners):
                back(chunk, 1, tile).wait_send()


def place_kernel(hot_ref, returned_ref, grad_ref):
    groups = returned_ref.shape[0]
    steps_win, tiles_dev, _ = grad_ref.shape
    rows = hot_ref.shape[0]
    view = returned_ref.reshape(groups, rows, LANES)
    hot = hot_ref[...]
    for group in range(0, groups, 2):
        pair = jnp.concatenate([view[group], view[group + 1]], axis=1)
        placed = lax.dot_general(
            hot, pair, (((0,), (0,)), ((), ())), preferred_element_type=jnp.float32
        )
        grad_ref[:, :, group * LANES:(group + 2) * LANES] = placed.reshape(steps_win, tiles_dev, 2 * LANES)


def on_device(flux, footprint, foot_slot, wanted, counts, observed, inv_var):
    steps_win, tiles_dev, cells = flux.shape
    _, soundings, per_sounding, _ = footprint.shape
    owners = lax.axis_size("tile")
    capacity = wanted.shape[3]
    own_rows = steps_win * tiles_dev
    entries = soundings * per_sounding
    groups = cells // LANES
    rows = 2 * owners * capacity
    wide = -(-own_rows // LANES) * LANES
    own = flux.reshape(steps_win, tiles_dev, groups, LANES).transpose(0, 2, 1, 3)
    prints = footprint.reshape(soundings, per_sounding, groups, LANES).transpose(0, 2, 1, 3)
    vmem = pl.BlockSpec(memory_space=pltpu.VMEM)
    smem = pl.BlockSpec(memory_space=pltpu.SMEM)
    hbm = pl.BlockSpec(memory_space=pl.ANY)
    dma = pltpu.SemaphoreType.DMA
    modeled, returned, hot = pl.pallas_call(
        exchange_kernel,
        out_shape=(
            jax.ShapeDtypeStruct((1, soundings), jnp.float32),
            jax.ShapeDtypeStruct((groups, 2 * owners, capacity, LANES), jnp.bfloat16),
            jax.ShapeDtypeStruct((rows, own_rows), jnp.bfloat16),
        ),
        in_specs=[hbm, hbm, vmem, smem, smem, vmem, vmem],
        out_specs=(vmem, vmem, vmem),
        scratch_shapes=[
            pltpu.VMEM((groups, steps_win, tiles_dev, LANES), jnp.bfloat16),
            pltpu.VMEM((groups, soundings, per_sounding, LANES), jnp.bfloat16),
            pltpu.VMEM((groups, 2 * owners, capacity, LANES), jnp.bfloat16),
            pltpu.VMEM((groups, 2 * owners, capacity, LANES), jnp.bfloat16),
            pltpu.VMEM((groups, owners, capacity, LANES), jnp.bfloat16),
            pltpu.VMEM((2, owners, rows, wide), jnp.int32),
            pltpu.VMEM((2 * owners, rows, wide), jnp.int32),
            pltpu.VMEM((rows, entries), jnp.float32),
            dma((CHUNKS,)),
            dma((CHUNKS,)),
            dma((2, CHUNKS)),
            dma((2 * owners,)),
            dma((2 * owners,)),
            dma((CHUNKS, 2 * owners)),
            dma((CHUNKS, 2 * owners)),
            dma((CHUNKS, 2 * owners)),
            dma((CHUNKS, 2 * owners)),
        ],
        compiler_params=pltpu.CompilerParams(collective_id=0, has_side_effects=True),
        name="exchange",
    )(
        own, prints, foot_slot[0].T, wanted[0, 0].T, counts[0], observed, inv_var,
    )
    per_block = groups // BLOCKS
    grad = pl.pallas_call(
        place_kernel,
        grid=(BLOCKS,),
        out_shape=jax.ShapeDtypeStruct((steps_win, tiles_dev, cells), jnp.float32),
        in_specs=[
            pl.BlockSpec((rows, own_rows), lambda block: (0, 0)),
            pl.BlockSpec((per_block, 2 * owners, capacity, LANES), lambda block: (block, 0, 0, 0)),
        ],
        out_specs=pl.BlockSpec((steps_win, tiles_dev, per_block * LANES), lambda block: (0, 0, block)),
        name="place",
    )(hot, returned)
    return modeled, grad


def solution(mesh):
    placed = (
        P(("member", "tm"), "tile", None),
        P("tm", "tile", None, None),
        P("tm", "tile", None),
        P("tm", "tile", None, None),
        P("tm", "tile", None),
        P("tm", "tile"),
        P("tm", "tile"),
    )
    return jax.shard_map(
        on_device,
        mesh=mesh,
        in_specs=placed,
        out_specs=(P(("member", "tm"), "tile"), P(("member", "tm"), "tile", None)),
        check_vma=False,
    )
```

```python
import jax
import jax.numpy as jnp
from jax import lax
from jax.experimental import pallas as pl
from jax.experimental.pallas import tpu as pltpu
from jax.sharding import PartitionSpec as P

MESH = pl.DeviceIdType.MESH
LANES = 128
OUT_SHARES = (2, 5, 5, 3, 1)
BACK_SHARES = (1, 3, 6, 6)
BLOCKS = 8


def spans(groups, shares):
    edges = [2 * (groups // 2 * sum(shares[:k]) // sum(shares)) for k in range(len(shares) + 1)]
    return [(low, high - low) for low, high in zip(edges, edges[1:])]


def exchange_kernel(
    own_hbm, prints_hbm, slots_ref, wanted_ref, counts_ref, observed_ref, inv_var_ref,
    modeled_ref, returned_ref, hot_ref,
    own_buf, prints_buf, send_buf, recv_buf, adj_buf, asks, asked, scores, mask, spread,
    own_sem, prints_sem, self_out, self_back, ask_send, ask_recv, out_send, out_recv, back_send, back_recv,
):
    windows, owners = lax.axis_size("tm"), lax.axis_size("tile")
    win, me = lax.axis_index("tm"), lax.axis_index("tile")
    steps_win, groups, tiles_dev, _ = own_hbm.shape
    soundings, _, per_sounding, _ = prints_hbm.shape
    capacity = wanted_ref.shape[0]
    own_rows = steps_win * tiles_dev
    entries = soundings * per_sounding
    slots = owners * capacity
    rows = 2 * slots
    out_parts, back_parts = spans(groups, OUT_SHARES), spans(groups, BACK_SHARES)
    has_before, has_after = win > 0, win < windows - 1

    own_rows_view = own_buf.reshape(groups, own_rows, LANES)
    prints_view = prints_buf.reshape(groups, entries, LANES)
    send_view = send_buf.reshape(groups, rows, LANES)
    recv_view = recv_buf.reshape(groups, rows, LANES)
    adj_view = adj_buf.reshape(groups, slots, LANES)
    returned_view = returned_ref.reshape(groups, rows, LANES)

    def out_span(chunk):
        return pl.ds(*out_parts[chunk])

    def back_span(chunk):
        return pl.ds(*back_parts[chunk])

    def load(source, target, semaphore):
        for chunk, (low, size) in enumerate(out_parts):
            @pl.loop(low, low + size)
            def _(group):
                pltpu.make_async_copy(source.at[:, group], target.at[group], semaphore.at[chunk]).start()

    def remote(source, target, send, recv, window, tile):
        return pltpu.make_async_remote_copy(
            src_ref=source, dst_ref=target, send_sem=send, recv_sem=recv,
            device_id={"tm": window, "tile": tile}, device_id_type=MESH,
        )

    def others(step):
        for away in range(1, owners):
            step(lax.rem(me + away, owners))

    barrier = pltpu.get_barrier_semaphore()

    def greet(window, tile):
        pl.semaphore_signal(barrier, inc=1, device_id={"tm": window, "tile": tile}, device_id_type=MESH)

    others(lambda tile: greet(win, tile))

    @pl.when(has_before)
    def _():
        for tile in range(owners):
            greet(win - 1, tile)

    @pl.when(has_after)
    def _():
        for tile in range(owners):
            greet(win + 1, tile)

    row_id = lax.broadcasted_iota(jnp.int32, asks.shape[2:], 0)
    for tile in range(owners):
        for late in range(2):
            block = jnp.full(asks.shape[2:], -1, jnp.int32)
            for place in range(capacity):
                value = wanted_ref[place, tile] - (0 if late else own_rows)
                block = jnp.where(row_id == (late * owners + me) * capacity + place, value, block)
            asks[late, tile] = block

    load(own_hbm, own_buf, own_sem)
    near = lax.div(win + windows - 1, windows) + lax.div(2 * windows - 2 - win, windows)
    pl.semaphore_wait(barrier, owners - 1 + owners * near)

    def ask(late, tile):
        return remote(
            asks.at[late, tile], asked.at[late * owners + me],
            ask_send.at[late * owners + tile], ask_recv.at[late * owners + me], win - late, tile,
        )

    def ask_from(late, tile):
        return remote(
            asks.at[late, tile], asked.at[late * owners + tile],
            ask_send.at[late * owners + tile], ask_recv.at[late * owners + tile], win, me,
        )

    @pl.when(has_before)
    def _():
        for tile in range(owners):
            ask(1, tile).start()

    others(lambda tile: ask(0, tile).start())
    asked[me] = asks[0, me]

    @pl.when(jnp.logical_not(has_after))
    def _():
        asked[owners:] = jnp.full((owners,) + asked.shape[1:], -1, jnp.int32)

    @pl.when(jnp.logical_not(has_before))
    def _():
        @pl.loop(0, groups)
        def _(group):
            recv_buf[group, owners:] = jnp.zeros((owners, capacity, LANES), jnp.bfloat16)

    load(prints_hbm, prints_buf, prints_sem)

    low = lax.broadcasted_iota(jnp.int32, (soundings, entries), 0) * per_sounding
    column = lax.broadcasted_iota(jnp.int32, (soundings, entries), 1)
    spread_of = ((column >= low) & (column < low + per_sounding)).astype(jnp.float32)
    spread[...] = spread_of
    each = jnp.dot(
        slots_ref[...].astype(jnp.float32), spread_of,
        precision=lax.Precision.HIGHEST, preferred_element_type=jnp.float32,
    )
    nth = lax.broadcasted_iota(jnp.int32, (per_sounding, entries), 0)
    at = lax.rem(lax.broadcasted_iota(jnp.int32, (per_sounding, entries), 1), per_sounding)
    entry = jnp.sum(jnp.where(nth == at, each, 0.0), axis=0, keepdims=True)
    slot_id = lax.broadcasted_iota(jnp.int32, (slots, entries), 0)
    have = jnp.zeros((slots, entries), jnp.int32)
    for tile in range(owners):
        have = jnp.where(slot_id // capacity == tile, counts_ref[0, tile], have)
    select = (slot_id.astype(jnp.float32) == entry) & (lax.rem(slot_id, capacity) < have)
    mask[...] = jnp.where(select, 1.0, 0.0)

    others(lambda tile: ask_from(0, tile).wait_recv())

    @pl.when(has_after)
    def _():
        for tile in range(owners):
            ask_from(1, tile).wait_recv()

    value = asked[0]
    for index in range(1, 2 * owners):
        value = jnp.maximum(value, asked[index])
    value = value[:, :own_rows]
    hot = (value == lax.broadcasted_iota(jnp.int32, value.shape, 1)).astype(jnp.float32).astype(jnp.bfloat16)
    hot_ref[...] = hot.astype(jnp.float32).T.astype(jnp.bfloat16)

    def out(chunk, late, tile):
        return remote(
            send_buf.at[out_span(chunk), late * owners + tile], recv_buf.at[out_span(chunk), late * owners + me],
            out_send.at[chunk, late * owners + tile], out_recv.at[chunk, late * owners + me], win + late, tile,
        )

    def out_from(chunk, late, tile):
        return remote(
            send_buf.at[out_span(chunk), late * owners + tile], recv_buf.at[out_span(chunk), late * owners + tile],
            out_send.at[chunk, late * owners + tile], out_recv.at[chunk, late * owners + tile], win, me,
        )

    def out_self(chunk):
        return pltpu.make_async_copy(
            send_buf.at[out_span(chunk), me], recv_buf.at[out_span(chunk), me], self_out.at[chunk]
        )

    for chunk, (low, size) in enumerate(out_parts):
        own_part = own_buf.at[out_span(chunk)]
        pltpu.make_async_copy(own_part, own_part, own_sem.at[chunk]).wait()

        @pl.loop(low // 2, (low + size) // 2, unroll=4)
        def _(step):
            group = 2 * step
            pair = jnp.concatenate([own_rows_view[group], own_rows_view[group + 1]], axis=1)
            picked = jnp.dot(hot, pair, preferred_element_type=jnp.float32).astype(jnp.bfloat16)
            send_view[group] = picked[:, :LANES]
            send_view[group + 1] = picked[:, LANES:]

        @pl.when(has_after)
        def _():
            for tile in range(owners):
                out(chunk, 1, tile).start()

        others(lambda tile: out(chunk, 0, tile).start())
        out_self(chunk).start()

    scores[...] = jnp.zeros_like(scores)

    for chunk, (low, size) in enumerate(out_parts):
        prints_part = prints_buf.at[out_span(chunk)]
        pltpu.make_async_copy(prints_part, prints_part, prints_sem.at[chunk]).wait()
        others(lambda tile: out_from(chunk, 0, tile).wait_recv())
        out_self(chunk).wait()

        @pl.when(has_before)
        def _():
            for tile in range(owners):
                out_from(chunk, 1, tile).wait_recv()

        def score(step, total):
            group = 2 * step
            pair = jnp.concatenate([prints_view[group], prints_view[group + 1]], axis=1)
            held = jnp.concatenate([recv_view[group], recv_view[group + 1]], axis=1)
            return total + lax.dot_general(
                held, pair, (((1,), (1,)), ((), ())), preferred_element_type=jnp.float32
            )

        scores[...] = lax.fori_loop(low // 2, (low + size) // 2, score, scores[...], unroll=4)

    select, spread_of = mask[...] > 0.0, spread[...]
    both = scores[:slots, :] + scores[slots:, :]
    entry_sums = jnp.sum(jnp.where(select, both, 0.0), axis=0, keepdims=True)
    modeled = lax.dot_general(
        jnp.broadcast_to(entry_sums, (8, entries)), spread_of, (((1,), (1,)), ((), ())),
        precision=lax.Precision.HIGHEST, preferred_element_type=jnp.float32,
    )
    modeled_ref[...] = modeled[:1]
    coef = ((modeled - observed_ref[...]) * inv_var_ref[...]).astype(jnp.bfloat16)
    coef_each = jnp.dot(coef, spread_of.astype(jnp.bfloat16), preferred_element_type=jnp.float32)[:1]
    weights = jnp.where(select, coef_each, 0.0).astype(jnp.bfloat16)

    def back(chunk, late, tile):
        return remote(
            adj_buf.at[back_span(chunk), tile], returned_ref.at[back_span(chunk), late * owners + me],
            back_send.at[chunk, late * owners + tile], back_recv.at[chunk, late * owners + me], win - late, tile,
        )

    def back_from(chunk, late, tile):
        return remote(
            adj_buf.at[back_span(chunk), tile], returned_ref.at[back_span(chunk), late * owners + tile],
            back_send.at[chunk, late * owners + tile], back_recv.at[chunk, late * owners + tile], win, me,
        )

    def back_self(chunk):
        return pltpu.make_async_copy(
            adj_buf.at[back_span(chunk), me], returned_ref.at[back_span(chunk), me], self_back.at[chunk]
        )

    for chunk, (low, size) in enumerate(back_parts):
        @pl.loop(low // 2, (low + size) // 2, unroll=4)
        def _(step):
            group = 2 * step
            pair = jnp.concatenate([prints_view[group], prints_view[group + 1]], axis=1)
            adjoint = jnp.dot(weights, pair, preferred_element_type=jnp.float32).astype(jnp.bfloat16)
            adj_view[group] = adjoint[:, :LANES]
            adj_view[group + 1] = adjoint[:, LANES:]

        @pl.when(has_before)
        def _():
            for tile in range(owners):
                back(chunk, 1, tile).start()

        others(lambda tile: back(chunk, 0, tile).start())
        back_self(chunk).start()

    @pl.when(jnp.logical_not(has_after))
    def _():
        @pl.loop(0, groups)
        def _(group):
            returned_ref[group, owners:] = jnp.zeros((owners, capacity, LANES), jnp.bfloat16)

    others(lambda tile: ask(0, tile).wait_send())

    @pl.when(has_before)
    def _():
        for tile in range(owners):
            ask(1, tile).wait_send()

    for chunk in range(len(out_parts)):
        others(lambda tile: out(chunk, 0, tile).wait_send())

        @pl.when(has_after)
        def _():
            for tile in range(owners):
                out(chunk, 1, tile).wait_send()

    for chunk in range(len(back_parts)):
        others(lambda tile: back(chunk, 0, tile).wait_send())
        others(lambda tile: back_from(chunk, 0, tile).wait_recv())
        back_self(chunk).wait()

        @pl.when(has_after)
        def _():
            for tile in range(owners):
                back_from(chunk, 1, tile).wait_recv()

        @pl.when(has_before)
        def _():
            for tile in range(owners):
                back(chunk, 1, tile).wait_send()


def place_kernel(hot_ref, returned_ref, modeled_ref, grad_hbm, modeled_out, grad_buf, grad_sem):
    groups = returned_ref.shape[0]
    steps_win, tiles_dev, _ = grad_buf.shape
    rows = hot_ref.shape[1]
    view = returned_ref.reshape(groups, rows, LANES)
    hot = hot_ref[...]
    modeled_out[...] = modeled_ref[...]
    copies = []
    for block, (low, size) in enumerate(spans(groups, (1,) * BLOCKS)):
        for group in range(low, low + size, 2):
            pair = jnp.concatenate([view[group], view[group + 1]], axis=1)
            placed = jnp.dot(hot, pair, preferred_element_type=jnp.float32)
            grad_buf[:, :, group * LANES:(group + 2) * LANES] = placed.reshape(steps_win, tiles_dev, 2 * LANES)
        cells = pl.ds(low * LANES, size * LANES)
        copies.append(pltpu.make_async_copy(grad_buf.at[:, :, cells], grad_hbm.at[:, :, cells], grad_sem.at[block]))
        copies[-1].start()
    for copy in copies:
        copy.wait()


def on_device(flux, footprint, foot_slot, wanted, counts, observed, inv_var):
    steps_win, tiles_dev, cells = flux.shape
    _, soundings, per_sounding, _ = footprint.shape
    owners = lax.axis_size("tile")
    capacity = wanted.shape[3]
    own_rows = steps_win * tiles_dev
    entries = soundings * per_sounding
    groups = cells // LANES
    rows = 2 * owners * capacity
    wide = -(-own_rows // LANES) * LANES
    own = flux.reshape(steps_win, tiles_dev, groups, LANES).transpose(0, 2, 1, 3)
    prints = footprint.reshape(soundings, per_sounding, groups, LANES).transpose(0, 2, 1, 3)
    vmem = pl.BlockSpec(memory_space=pltpu.VMEM)
    smem = pl.BlockSpec(memory_space=pltpu.SMEM)
    hbm = pl.BlockSpec(memory_space=pl.ANY)
    dma = pltpu.SemaphoreType.DMA
    modeled, returned, hot = pl.pallas_call(
        exchange_kernel,
        out_shape=(
            jax.ShapeDtypeStruct((1, soundings), jnp.float32),
            jax.ShapeDtypeStruct((groups, 2 * owners, capacity, LANES), jnp.bfloat16),
            jax.ShapeDtypeStruct((own_rows, rows), jnp.bfloat16),
        ),
        in_specs=[hbm, hbm, vmem, smem, smem, vmem, vmem],
        out_specs=(vmem, vmem, vmem),
        scratch_shapes=[
            pltpu.VMEM((groups, steps_win, tiles_dev, LANES), jnp.bfloat16),
            pltpu.VMEM((groups, soundings, per_sounding, LANES), jnp.bfloat16),
            pltpu.VMEM((groups, 2 * owners, capacity, LANES), jnp.bfloat16),
            pltpu.VMEM((groups, 2 * owners, capacity, LANES), jnp.bfloat16),
            pltpu.VMEM((groups, owners, capacity, LANES), jnp.bfloat16),
            pltpu.VMEM((2, owners, rows, wide), jnp.int32),
            pltpu.VMEM((2 * owners, rows, wide), jnp.int32),
            pltpu.VMEM((rows, entries), jnp.float32),
            pltpu.VMEM((owners * capacity, entries), jnp.float32),
            pltpu.VMEM((soundings, entries), jnp.float32),
            dma((len(OUT_SHARES),)),
            dma((len(OUT_SHARES),)),
            dma((len(OUT_SHARES),)),
            dma((len(BACK_SHARES),)),
            dma((2 * owners,)),
            dma((2 * owners,)),
            dma((len(OUT_SHARES), 2 * owners)),
            dma((len(OUT_SHARES), 2 * owners)),
            dma((len(BACK_SHARES), 2 * owners)),
            dma((len(BACK_SHARES), 2 * owners)),
        ],
        compiler_params=pltpu.CompilerParams(collective_id=0, has_side_effects=True),
        name="exchange",
    )(
        own, prints, foot_slot[0].T, wanted[0, 0].T, counts[0], observed, inv_var,
    )
    grad, modeled = pl.pallas_call(
        place_kernel,
        out_shape=(
            jax.ShapeDtypeStruct((steps_win, tiles_dev, cells), jnp.float32),
            jax.ShapeDtypeStruct((1, soundings), jnp.float32),
        ),
        in_specs=[vmem, vmem, vmem],
        out_specs=(hbm, vmem),
        scratch_shapes=[pltpu.VMEM((steps_win, tiles_dev, cells), jnp.float32), dma((BLOCKS,))],
        name="place",
    )(hot, returned, modeled)
    return modeled, grad


def solution(mesh):
    placed = (
        P(("member", "tm"), "tile", None),
        P("tm", "tile", None, None),
        P("tm", "tile", None),
        P("tm", "tile", None, None),
        P("tm", "tile", None),
        P("tm", "tile"),
        P("tm", "tile"),
    )
    return jax.shard_map(
        on_device,
        mesh=mesh,
        in_specs=placed,
        out_specs=(P(("member", "tm"), "tile"), P(("member", "tm"), "tile", None)),
        check_vma=False,
    )
```

```python
import jax
import jax.numpy as jnp
from jax import lax
from jax.experimental import pallas as pl
from jax.experimental.pallas import tpu as pltpu
from jax.sharding import PartitionSpec as P

MESH = pl.DeviceIdType.MESH
LANES = 128
OUT_SHARES = (2, 5, 5, 3, 1)
BACK_SHARES = (1, 3, 6, 6)
BLOCKS = 8


def spans(groups, shares):
    edges = [2 * (groups // 2 * sum(shares[:k]) // sum(shares)) for k in range(len(shares) + 1)]
    return [(low, high - low) for low, high in zip(edges, edges[1:])]


def exchange_kernel(
    own_hbm, prints_hbm, slots_ref, wanted_ref, counts_ref, observed_ref, inv_var_ref,
    modeled_ref, returned_ref, hot_ref,
    own_buf, prints_buf, send_buf, recv_buf, adj_buf, asks, asked, scores, mask, spread,
    own_sem, prints_sem, self_out, self_back, ask_send, ask_recv, out_send, out_recv, back_send, back_recv,
):
    windows, owners = lax.axis_size("tm"), lax.axis_size("tile")
    win, me = lax.axis_index("tm"), lax.axis_index("tile")
    steps_win, groups, tiles_dev, _ = own_hbm.shape
    soundings, _, per_sounding, _ = prints_hbm.shape
    capacity = wanted_ref.shape[0]
    own_rows = steps_win * tiles_dev
    entries = soundings * per_sounding
    slots = owners * capacity
    rows = 2 * slots
    out_parts, back_parts = spans(groups, OUT_SHARES), spans(groups, BACK_SHARES)
    has_before, has_after = win > 0, win < windows - 1

    own_rows_view = own_buf.reshape(groups, own_rows, LANES)
    prints_view = prints_buf.reshape(groups, entries, LANES)
    send_view = send_buf.reshape(groups, rows, LANES)
    recv_view = recv_buf.reshape(groups, rows, LANES)
    adj_view = adj_buf.reshape(groups, slots, LANES)
    returned_view = returned_ref.reshape(groups, rows, LANES)

    def out_span(chunk):
        return pl.ds(*out_parts[chunk])

    def back_span(chunk):
        return pl.ds(*back_parts[chunk])

    def load(source, target, semaphore):
        for chunk, (low, size) in enumerate(out_parts):
            @pl.loop(low, low + size)
            def _(group):
                pltpu.make_async_copy(source.at[:, group], target.at[group], semaphore.at[chunk]).start()

    def remote(source, target, send, recv, window, tile):
        return pltpu.make_async_remote_copy(
            src_ref=source, dst_ref=target, send_sem=send, recv_sem=recv,
            device_id={"tm": window, "tile": tile}, device_id_type=MESH,
        )

    def others(step):
        for away in range(1, owners):
            step(lax.rem(me + away, owners))

    barrier = pltpu.get_barrier_semaphore()

    def greet(window, tile):
        pl.semaphore_signal(barrier, inc=1, device_id={"tm": window, "tile": tile}, device_id_type=MESH)

    others(lambda tile: greet(win, tile))

    @pl.when(has_before)
    def _():
        for tile in range(owners):
            greet(win - 1, tile)

    @pl.when(has_after)
    def _():
        for tile in range(owners):
            greet(win + 1, tile)

    row_id = lax.broadcasted_iota(jnp.int32, asks.shape[2:], 1)
    for tile in range(owners):
        for late in range(2):
            block = jnp.full(asks.shape[2:], -1, jnp.int32)
            for place in range(capacity):
                value = wanted_ref[place, tile] - (0 if late else own_rows)
                block = jnp.where(row_id == (late * owners + me) * capacity + place, value, block)
            asks[late, tile] = block

    load(own_hbm, own_buf, own_sem)
    near = lax.div(win + windows - 1, windows) + lax.div(2 * windows - 2 - win, windows)
    pl.semaphore_wait(barrier, owners - 1 + owners * near)

    def ask(late, tile):
        return remote(
            asks.at[late, tile], asked.at[late * owners + me],
            ask_send.at[late * owners + tile], ask_recv.at[late * owners + me], win - late, tile,
        )

    def ask_from(late, tile):
        return remote(
            asks.at[late, tile], asked.at[late * owners + tile],
            ask_send.at[late * owners + tile], ask_recv.at[late * owners + tile], win, me,
        )

    @pl.when(has_before)
    def _():
        for tile in range(owners):
            ask(1, tile).start()

    others(lambda tile: ask(0, tile).start())
    asked[me] = asks[0, me]

    @pl.when(jnp.logical_not(has_after))
    def _():
        asked[owners:] = jnp.full((owners,) + asked.shape[1:], -1, jnp.int32)

    @pl.when(jnp.logical_not(has_before))
    def _():
        @pl.loop(0, groups)
        def _(group):
            recv_buf[group, owners:] = jnp.zeros((owners, capacity, LANES), jnp.bfloat16)

    load(prints_hbm, prints_buf, prints_sem)

    low = lax.broadcasted_iota(jnp.int32, (soundings, entries), 0) * per_sounding
    column = lax.broadcasted_iota(jnp.int32, (soundings, entries), 1)
    spread_of = ((column >= low) & (column < low + per_sounding)).astype(jnp.float32)
    spread[...] = spread_of
    each = jnp.dot(
        slots_ref[...].astype(jnp.float32), spread_of,
        precision=lax.Precision.HIGHEST, preferred_element_type=jnp.float32,
    )
    nth = lax.broadcasted_iota(jnp.int32, (per_sounding, entries), 0)
    at = lax.rem(lax.broadcasted_iota(jnp.int32, (per_sounding, entries), 1), per_sounding)
    entry = jnp.sum(jnp.where(nth == at, each, 0.0), axis=0, keepdims=True)
    slot_id = lax.broadcasted_iota(jnp.int32, (slots, entries), 0)
    have = jnp.zeros((slots, entries), jnp.int32)
    for tile in range(owners):
        have = jnp.where(slot_id // capacity == tile, counts_ref[0, tile], have)
    select = (slot_id.astype(jnp.float32) == entry) & (lax.rem(slot_id, capacity) < have)
    mask[...] = jnp.where(select, 1.0, 0.0)

    others(lambda tile: ask_from(0, tile).wait_recv())

    @pl.when(has_after)
    def _():
        for tile in range(owners):
            ask_from(1, tile).wait_recv()

    value = asked[0]
    for index in range(1, 2 * owners):
        value = jnp.maximum(value, asked[index])
    own_id = lax.broadcasted_iota(jnp.int32, (own_rows, rows), 0)
    places = (value[:, :rows] == own_id).astype(jnp.float32)
    hot_ref[...] = places.astype(jnp.bfloat16)
    hot = places.T.astype(jnp.bfloat16)

    def out(chunk, late, tile):
        return remote(
            send_buf.at[out_span(chunk), late * owners + tile], recv_buf.at[out_span(chunk), late * owners + me],
            out_send.at[chunk, late * owners + tile], out_recv.at[chunk, late * owners + me], win + late, tile,
        )

    def out_from(chunk, late, tile):
        return remote(
            send_buf.at[out_span(chunk), late * owners + tile], recv_buf.at[out_span(chunk), late * owners + tile],
            out_send.at[chunk, late * owners + tile], out_recv.at[chunk, late * owners + tile], win, me,
        )

    def out_self(chunk):
        return pltpu.make_async_copy(
            send_buf.at[out_span(chunk), me], recv_buf.at[out_span(chunk), me], self_out.at[chunk]
        )

    for chunk, (low, size) in enumerate(out_parts):
        own_part = own_buf.at[out_span(chunk)]
        pltpu.make_async_copy(own_part, own_part, own_sem.at[chunk]).wait()

        @pl.loop(low // 2, (low + size) // 2, unroll=size // 4)
        def _(step):
            group = 2 * step
            pair = jnp.concatenate([own_rows_view[group], own_rows_view[group + 1]], axis=1)
            picked = jnp.dot(hot, pair, preferred_element_type=jnp.float32).astype(jnp.bfloat16)
            send_view[group] = picked[:, :LANES]
            send_view[group + 1] = picked[:, LANES:]

        @pl.when(has_after)
        def _():
            for tile in range(owners):
                out(chunk, 1, tile).start()

        others(lambda tile: out(chunk, 0, tile).start())
        out_self(chunk).start()

    scores[...] = jnp.zeros_like(scores)

    for chunk, (low, size) in enumerate(out_parts):
        prints_part = prints_buf.at[out_span(chunk)]
        pltpu.make_async_copy(prints_part, prints_part, prints_sem.at[chunk]).wait()
        others(lambda tile: out_from(chunk, 0, tile).wait_recv())
        out_self(chunk).wait()

        @pl.when(has_before)
        def _():
            for tile in range(owners):
                out_from(chunk, 1, tile).wait_recv()

        def score(step, total):
            group = 2 * step
            pair = jnp.concatenate([prints_view[group], prints_view[group + 1]], axis=1)
            held = jnp.concatenate([recv_view[group], recv_view[group + 1]], axis=1)
            return total + lax.dot_general(
                held, pair, (((1,), (1,)), ((), ())), preferred_element_type=jnp.float32
            )

        scores[...] = lax.fori_loop(low // 2, (low + size) // 2, score, scores[...], unroll=size // 4)

    select, spread_of = mask[...] > 0.0, spread[...]
    both = scores[:slots, :] + scores[slots:, :]
    entry_sums = jnp.sum(jnp.where(select, both, 0.0), axis=0, keepdims=True)
    modeled = lax.dot_general(
        jnp.broadcast_to(entry_sums, (8, entries)), spread_of, (((1,), (1,)), ((), ())),
        precision=lax.Precision.HIGHEST, preferred_element_type=jnp.float32,
    )
    modeled_ref[...] = modeled[:1]
    coef = ((modeled - observed_ref[...]) * inv_var_ref[...]).astype(jnp.bfloat16)
    coef_each = jnp.dot(coef, spread_of.astype(jnp.bfloat16), preferred_element_type=jnp.float32)[:1]
    weights = jnp.where(select, coef_each, 0.0).astype(jnp.bfloat16)

    def back(chunk, late, tile):
        return remote(
            adj_buf.at[back_span(chunk), tile], returned_ref.at[back_span(chunk), late * owners + me],
            back_send.at[chunk, late * owners + tile], back_recv.at[chunk, late * owners + me], win - late, tile,
        )

    def back_from(chunk, late, tile):
        return remote(
            adj_buf.at[back_span(chunk), tile], returned_ref.at[back_span(chunk), late * owners + tile],
            back_send.at[chunk, late * owners + tile], back_recv.at[chunk, late * owners + tile], win, me,
        )

    def back_self(chunk):
        return pltpu.make_async_copy(
            adj_buf.at[back_span(chunk), me], returned_ref.at[back_span(chunk), me], self_back.at[chunk]
        )

    for chunk, (low, size) in enumerate(back_parts):
        @pl.loop(low // 2, (low + size) // 2, unroll=size // 4)
        def _(step):
            group = 2 * step
            pair = jnp.concatenate([prints_view[group], prints_view[group + 1]], axis=1)
            adjoint = jnp.dot(weights, pair, preferred_element_type=jnp.float32).astype(jnp.bfloat16)
            adj_view[group] = adjoint[:, :LANES]
            adj_view[group + 1] = adjoint[:, LANES:]

        @pl.when(has_before)
        def _():
            for tile in range(owners):
                back(chunk, 1, tile).start()

        others(lambda tile: back(chunk, 0, tile).start())
        back_self(chunk).start()

    @pl.when(jnp.logical_not(has_after))
    def _():
        @pl.loop(0, groups)
        def _(group):
            returned_ref[group, owners:] = jnp.zeros((owners, capacity, LANES), jnp.bfloat16)

    others(lambda tile: ask(0, tile).wait_send())

    @pl.when(has_before)
    def _():
        for tile in range(owners):
            ask(1, tile).wait_send()

    for chunk in range(len(out_parts)):
        others(lambda tile: out(chunk, 0, tile).wait_send())

        @pl.when(has_after)
        def _():
            for tile in range(owners):
                out(chunk, 1, tile).wait_send()

    for chunk in range(len(back_parts)):
        others(lambda tile: back(chunk, 0, tile).wait_send())
        others(lambda tile: back_from(chunk, 0, tile).wait_recv())
        back_self(chunk).wait()

        @pl.when(has_after)
        def _():
            for tile in range(owners):
                back_from(chunk, 1, tile).wait_recv()

        @pl.when(has_before)
        def _():
            for tile in range(owners):
                back(chunk, 1, tile).wait_send()


def place_kernel(hot_ref, returned_ref, modeled_ref, grad_hbm, modeled_out, grad_buf, grad_sem):
    groups = returned_ref.shape[0]
    steps_win, tiles_dev, _ = grad_buf.shape
    rows = hot_ref.shape[1]
    view = returned_ref.reshape(groups, rows, LANES)
    hot = hot_ref[...]
    modeled_out[...] = modeled_ref[...]
    copies = []
    for block, (low, size) in enumerate(spans(groups, (1,) * BLOCKS)):
        for group in range(low, low + size, 2):
            pair = jnp.concatenate([view[group], view[group + 1]], axis=1)
            placed = jnp.dot(hot, pair, preferred_element_type=jnp.float32)
            grad_buf[:, :, group * LANES:(group + 2) * LANES] = placed.reshape(steps_win, tiles_dev, 2 * LANES)
        cells = pl.ds(low * LANES, size * LANES)
        copies.append(pltpu.make_async_copy(grad_buf.at[:, :, cells], grad_hbm.at[:, :, cells], grad_sem.at[block]))
        copies[-1].start()
    for copy in copies:
        copy.wait()


def on_device(flux, footprint, foot_slot, wanted, counts, observed, inv_var):
    steps_win, tiles_dev, cells = flux.shape
    _, soundings, per_sounding, _ = footprint.shape
    owners = lax.axis_size("tile")
    capacity = wanted.shape[3]
    own_rows = steps_win * tiles_dev
    entries = soundings * per_sounding
    groups = cells // LANES
    rows = 2 * owners * capacity
    wide = -(-rows // LANES) * LANES
    own = flux.reshape(steps_win, tiles_dev, groups, LANES).transpose(0, 2, 1, 3)
    prints = footprint.reshape(soundings, per_sounding, groups, LANES).transpose(0, 2, 1, 3)
    vmem = pl.BlockSpec(memory_space=pltpu.VMEM)
    smem = pl.BlockSpec(memory_space=pltpu.SMEM)
    hbm = pl.BlockSpec(memory_space=pl.ANY)
    dma = pltpu.SemaphoreType.DMA
    modeled, returned, hot = pl.pallas_call(
        exchange_kernel,
        out_shape=(
            jax.ShapeDtypeStruct((1, soundings), jnp.float32),
            jax.ShapeDtypeStruct((groups, 2 * owners, capacity, LANES), jnp.bfloat16),
            jax.ShapeDtypeStruct((own_rows, rows), jnp.bfloat16),
        ),
        in_specs=[hbm, hbm, vmem, smem, smem, vmem, vmem],
        out_specs=(vmem, vmem, vmem),
        scratch_shapes=[
            pltpu.VMEM((groups, steps_win, tiles_dev, LANES), jnp.bfloat16),
            pltpu.VMEM((groups, soundings, per_sounding, LANES), jnp.bfloat16),
            pltpu.VMEM((groups, 2 * owners, capacity, LANES), jnp.bfloat16),
            pltpu.VMEM((groups, 2 * owners, capacity, LANES), jnp.bfloat16),
            pltpu.VMEM((groups, owners, capacity, LANES), jnp.bfloat16),
            pltpu.VMEM((2, owners, 1, wide), jnp.int32),
            pltpu.VMEM((2 * owners, 1, wide), jnp.int32),
            pltpu.VMEM((rows, entries), jnp.float32),
            pltpu.VMEM((owners * capacity, entries), jnp.float32),
            pltpu.VMEM((soundings, entries), jnp.float32),
            dma((len(OUT_SHARES),)),
            dma((len(OUT_SHARES),)),
            dma((len(OUT_SHARES),)),
            dma((len(BACK_SHARES),)),
            dma((2 * owners,)),
            dma((2 * owners,)),
            dma((len(OUT_SHARES), 2 * owners)),
            dma((len(OUT_SHARES), 2 * owners)),
            dma((len(BACK_SHARES), 2 * owners)),
            dma((len(BACK_SHARES), 2 * owners)),
        ],
        compiler_params=pltpu.CompilerParams(collective_id=0, has_side_effects=True),
        name="exchange",
    )(
        own, prints, foot_slot[0].T, wanted[0, 0].T, counts[0], observed, inv_var,
    )
    grad, modeled = pl.pallas_call(
        place_kernel,
        out_shape=(
            jax.ShapeDtypeStruct((steps_win, tiles_dev, cells), jnp.float32),
            jax.ShapeDtypeStruct((1, soundings), jnp.float32),
        ),
        in_specs=[vmem, vmem, vmem],
        out_specs=(hbm, vmem),
        scratch_shapes=[pltpu.VMEM((steps_win, tiles_dev, cells), jnp.float32), dma((BLOCKS,))],
        name="place",
    )(hot, returned, modeled)
    return modeled, grad


def solution(mesh):
    placed = (
        P(("member", "tm"), "tile", None),
        P("tm", "tile", None, None),
        P("tm", "tile", None),
        P("tm", "tile", None, None),
        P("tm", "tile", None),
        P("tm", "tile"),
        P("tm", "tile"),
    )
    return jax.shard_map(
        on_device,
        mesh=mesh,
        in_specs=placed,
        out_specs=(P(("member", "tm"), "tile"), P(("member", "tm"), "tile", None)),
        check_vma=False,
    )
```
